32 devices in a mesh: groups: 2 (over x), tensor: 4 (over y, core), dp: 4 (over z).
Axes of the slice: x: 2, y: 2, z: 4, core: 2. Of those that a mesh axis runs over, the one named last changes fastest.
Arguments:
- first_out: bfloat16 [4096, 1024], P(('groups', 'tensor', 'dp')), parts along dimension 0, may hold values from -6 to 6
- second_out: bfloat16 [4096, 1024], P(('groups', 'tensor', 'dp')), parts along dimension 0, may hold values from -6 to 6
- grad_first: bfloat16 [4096, 1024], P(('groups', 'tensor', 'dp')), parts along dimension 0, may hold values from -6 to 6
- grad_second: bfloat16 [4096, 1024], P(('groups', 'tensor', 'dp')), parts along dimension 0, may hold values from -6 to 6
- w_up: bfloat16 [1024, 8192], P('dp', 'tensor'), may hold values from -0.1875 to 0.1875
- w_down: bfloat16 [8192, 1024], P('tensor', 'dp'), may hold values from -0.0625 to 0.0625
- norm_gain: float32 [1024], replicated, may hold values from 0.25 to 1.75
- norm_bias: float32 [1024], replicated, may hold values from -3 to 3
Outputs:
- second_in: bfloat16 [4096, 1024], P(('groups', 'tensor', 'dp')), parts along dimension 0
- grad_first_in: float32 [4096, 1024], P(('groups', 'tensor', 'dp')), parts along dimension 0
- grad_up: float32 [2048, 8192], P(('groups', 'dp'), 'tensor'), parts along dimension 0
- grad_down: float32 [16384, 1024], P(('groups', 'tensor'), 'dp'), parts along dimension 0
- grad_norm: float32 [4, 1024], P('groups'), parts along dimension 0
The draws below stay inside these ranges and needn't reach their ends.
There are 2 independent parts, one for each index of `groups`. The reference program is written for one: setup_inputs(seed, part) draws one part's arguments, and reference() takes and returns one part's arrays. A program takes and returns all parts, laid end to end along the dimension named above; an argument that names none is the same for every part. Nothing has to cross between parts.
All inputs are finite; a program needn't handle non-finite values.
Results may differ from the reference program's by a relative error of at most 0.017.
Values may be sent and summed in bfloat16 or wider, within the bound.
A program may use at most 64 MiB of HBM per device.

```python
import jax
import jax.numpy as jnp
from jax import lax

D = 1024
FF = 8192
TOKENS = 2048
N_TENSOR = 4


def block_scale(key, dims, split, least, top_value):
    level, own = 1.0, jax.random.fold_in(key, 6)
    for dim, shards_of in split:
        heights = jnp.exp(jax.random.uniform(jax.random.fold_in(own, dim), (shards_of,), jnp.float32, least / len(split), top_value / len(split)))
        level = level * jnp.repeat(heights, dims[dim] // shards_of).reshape([-1 if axis == dim else 1 for axis in range(len(dims))])
    return level


def noise(rng, extent, width, limit, shards=(), kind=jnp.bfloat16):
    loudness = block_scale(rng, extent, shards, -0.22, 0.18) if shards else 1.0
    result = jax.random.normal(rng, extent, jnp.float32) * width * loudness
    return jnp.minimum(jnp.maximum(result, -limit), limit).astype(kind)


def setup_inputs(seed: int = 0, part: int = 0) -> dict:
    splits = jax.random.split(jax.random.key(seed), 9)
    part_splits = jax.random.split(jax.random.fold_in(splits[8], part), 9)
    first_out = noise(part_splits[0], (TOKENS, D), 1.0, 6.0, ((0, 16),))
    second_out = noise(part_splits[1], (TOKENS, D), 1.0, 6.0, ((0, 16),))
    grad_first = noise(part_splits[2], (TOKENS, D), 1.0, 6.0, ((0, 16),))
    grad_second = noise(part_splits[3], (TOKENS, D), 1.0, 6.0, ((0, 16),))
    w_up = noise(splits[4], (D, FF), D ** -0.5, 0.1875, ((0, 4), (1, 4)))
    w_down = noise(splits[5], (FF, D), FF ** -0.5, 0.0625, ((0, 4), (1, 4)))
    norm_gain = jnp.clip(1.0 + 0.15 * jax.random.normal(splits[6], (D,), jnp.float32), 0.25, 1.75)
    norm_bias = noise(splits[7], (D,), 0.5, 3.0, (), jnp.float32)
    return dict(first_out=first_out, second_out=second_out, grad_first=grad_first, grad_second=grad_second, w_up=w_up, w_down=w_down, norm_gain=norm_gain, norm_bias=norm_bias)


epsilon = 1e-06

def normalize(row_data, norm_gain, norm_bias):
    values = row_data.astype(jnp.float32)
    row_mean = lax.optimization_barrier(jnp.mean(values, axis=-1, keepdims=True))
    centred = values - row_mean
    inv_std = lax.rsqrt(lax.optimization_barrier(jnp.mean(centred * centred, axis=-1, keepdims=True)) + epsilon)
    standard = centred * inv_std
    normed = (standard * norm_gain.astype(jnp.float32) + norm_bias.astype(jnp.float32)).astype(jnp.bfloat16)
    return (standard, inv_std, normed)

def round_half(values):
    return lax.optimization_barrier(values.astype(jnp.bfloat16)).astype(jnp.float32)

def reference(first_out, second_out, grad_first, grad_second, w_up, w_down, norm_gain, norm_bias):
    standard, inv_std, normed = normalize(first_out, norm_gain, norm_bias)
    block_width = FF // N_TENSOR
    up_blocks = jnp.transpose(w_up.reshape(D, N_TENSOR, block_width), (1, 0, 2))
    down_blocks = w_down.reshape(N_TENSOR, block_width, D)

    def step_block(totals, blocks):
        branch, grad_normed = totals
        up_block, down_block = blocks
        preact = jnp.dot(normed, up_block, preferred_element_type=jnp.float32)
        hidden = jax.nn.gelu(preact).astype(jnp.bfloat16)
        branch = branch + round_half(jnp.dot(hidden, down_block, preferred_element_type=jnp.float32))
        grad_hidden = lax.dot_general(grad_second, down_block, (((1,), (1,)), ((), ())), preferred_element_type=jnp.float32)
        grad_pre = jax.vjp(jax.nn.gelu, preact)[1](grad_hidden)[0].astype(jnp.bfloat16)
        grad_down = lax.dot_general(hidden, grad_second, (((0,), (0,)), ((), ())), preferred_element_type=jnp.float32)
        grad_up = lax.dot_general(normed, grad_pre, (((0,), (0,)), ((), ())), preferred_element_type=jnp.float32)
        grad_normed = grad_normed + round_half(lax.dot_general(grad_pre, up_block, (((1,), (1,)), ((), ())), preferred_element_type=jnp.float32))
        return ((branch, grad_normed), (grad_up, grad_down))
    empty_rows = jnp.zeros((TOKENS, D), jnp.float32)
    (branch, grad_normed), (up_grads, down_grads) = lax.scan(step_block, (empty_rows, empty_rows), (up_blocks, down_blocks))
    grad_scale = TOKENS ** (-0.5)
    second_in = (second_out.astype(jnp.float32) - branch).astype(jnp.bfloat16)
    grad_std = grad_normed * norm_gain.astype(jnp.float32)
    grad_rows = inv_std * (grad_std - lax.optimization_barrier(jnp.mean(grad_std, axis=-1, keepdims=True)) - standard * lax.optimization_barrier(jnp.mean(grad_std * standard, axis=-1, keepdims=True)))
    grad_first_in = grad_first.astype(jnp.float32) + grad_rows
    grad_norm = jnp.stack([lax.optimization_barrier(jnp.sum(grad_normed * standard, axis=0)), lax.optimization_barrier(jnp.sum(grad_normed, axis=0))]) * grad_scale
    grad_up = jnp.transpose(up_grads, (1, 0, 2)).reshape(D, FF) * grad_scale
    grad_down = down_grads.reshape(FF, D) * grad_scale
    return (second_in, grad_first_in, grad_up, grad_down, grad_norm)
```

```python
import functools

import jax
import jax.numpy as jnp
import numpy as np
from jax import lax
from jax.experimental import pallas as pl
from jax.experimental.pallas import tpu as pltpu
from jax.sharding import PartitionSpec as P

epsilon = 1e-06


def normalize(row_data, norm_gain, norm_bias):
    values = row_data.astype(jnp.float32)
    row_mean = jnp.mean(values, axis=-1, keepdims=True)
    centred = values - row_mean
    inv_std = lax.rsqrt(jnp.mean(centred * centred, axis=-1, keepdims=True) + epsilon)
    standard = centred * inv_std
    normed = (standard * norm_gain + norm_bias).astype(jnp.bfloat16)
    return (standard, inv_std, normed)


def contract_tokens(left_rows, right_rows):
    return lax.dot_general(
        left_rows, right_rows, (((0,), (0,)), ((), ())), preferred_element_type=jnp.float32
    )


def body(first_out, second_out, grad_first, grad_second, w_up, w_down, norm_gain, norm_bias):
    own_rows = first_out.shape[0]
    up_full, down_full = (
        lax.all_gather(w_up, "dp", axis=0, tiled=True),
        lax.all_gather(w_down, "dp", axis=1, tiled=True),
    )
    first_all, grad_all = (
        lax.all_gather(first_out, "tensor", axis=0, tiled=True),
        lax.all_gather(grad_second, "tensor", axis=0, tiled=True),
    )
    standard_all, inv_std_all, normed = normalize(first_all, norm_gain, norm_bias)
    offset = lax.axis_index("tensor") * own_rows
    standard = lax.dynamic_slice_in_dim(standard_all, offset, own_rows, 0)
    inv_std = lax.dynamic_slice_in_dim(inv_std_all, offset, own_rows, 0)
    preact = jnp.dot(normed, up_full, preferred_element_type=jnp.float32)
    hidden = jax.nn.gelu(preact).astype(jnp.bfloat16)
    branch = lax.psum_scatter(
        jnp.dot(hidden, down_full, preferred_element_type=jnp.float32).astype(jnp.bfloat16),
        "tensor",
        scatter_dimension=0,
        tiled=True,
    ).astype(jnp.float32)
    second_in = (second_out.astype(jnp.float32) - branch).astype(jnp.bfloat16)
    tokens = own_rows * lax.axis_size("tensor") * lax.axis_size("dp")
    grad_scale = tokens ** (-0.5)
    grad_down_part = contract_tokens(hidden, grad_all)
    grad_down = (
        lax.psum_scatter(
            grad_down_part.astype(jnp.bfloat16), "dp", scatter_dimension=1, tiled=True
        ).astype(jnp.float32)
        * grad_scale
    )
    grad_hidden = lax.dot_general(
        grad_all, down_full, (((1,), (1,)), ((), ())), preferred_element_type=jnp.float32
    )
    grad_pre = jax.vjp(jax.nn.gelu, preact)[1](grad_hidden)[0].astype(jnp.bfloat16)
    grad_up_part = contract_tokens(normed, grad_pre)
    grad_up = (
        lax.psum_scatter(
            grad_up_part.astype(jnp.bfloat16), "dp", scatter_dimension=0, tiled=True
        ).astype(jnp.float32)
        * grad_scale
    )
    grad_normed = lax.psum_scatter(
        lax.dot_general(
            grad_pre, up_full, (((1,), (1,)), ((), ())), preferred_element_type=jnp.float32
        ).astype(jnp.bfloat16),
        "tensor",
        scatter_dimension=0,
        tiled=True,
    ).astype(jnp.float32)
    grad_std = grad_normed * norm_gain
    grad_rows = inv_std * (
        grad_std
        - jnp.mean(grad_std, axis=-1, keepdims=True)
        - standard * jnp.mean(grad_std * standard, axis=-1, keepdims=True)
    )
    grad_first_in = grad_first.astype(jnp.float32) + grad_rows
    local_stats = jnp.stack([jnp.sum(grad_normed * standard, axis=0), jnp.sum(grad_normed, axis=0)])
    grad_norm = lax.psum(local_stats, ("tensor", "dp")) * grad_scale
    return (second_in, grad_first_in, grad_up, grad_down, grad_norm)


def span(index, size):
    return pl.ds(pl.multiple_of(index * size, size), size)


def flipped(index, mask, bits):
    for bit in range(bits):
        if mask >> bit & 1:
            step = 1 << bit
            index = index + (1 - 2 * ((index // step) % 2)) * step
    return index


def nearness(own, n_dp):
    return lambda z: (abs(z - own), z)


def earliness(own, n_dp):
    def key(z):
        edge = min(z, n_dp - 1 - z)
        return (z != own, edge, abs(z - own) if edge == 0 else -abs(z - own))

    return key


def ranked_place(dp, n_dp, rank, ranking=nearness):
    place = 0
    for own in range(n_dp):
        ranked = sorted(range(n_dp), key=ranking(own, n_dp))
        for k in range(n_dp):
            here = jnp.logical_and(dp == own, jnp.equal(rank, k))
            place = place + jnp.where(here, ranked[k], 0)
    return place


def remote(src, dst, sems, index, peer):
    return pltpu.make_async_remote_copy(
        src_ref=src,
        dst_ref=dst,
        send_sem=sems[0].at[index],
        recv_sem=sems[1].at[index],
        device_id=peer,
        device_id_type=pl.DeviceIdType.MESH,
    )


def standardize(row_data):
    values = row_data.astype(jnp.float32)
    centred = values - jnp.mean(values, axis=-1, keepdims=True)
    inv_std = lax.rsqrt(jnp.mean(centred * centred, axis=-1, keepdims=True) + epsilon)
    return centred * inv_std, inv_std


def fused_kernel(
    n_groups, n_tensor, n_dp, grad_scale,
    first_ref, second_ref, grad_first_in_ref, grad_ref, w_up_ref, w_down_ref, gain_ref, bias_ref,
    second_in_ref, grad_first_ref, grad_norm_ref, up_out, down_out,
    normed_all, grad_all, up_ref, down_ref, hidden_ref, slope_ref, pre_ref, g_up_ref, g_down_ref, own_normed,
    partials, fold, moving, stat_line, stat_fold, local_sem,
    row_send, row_recv, column_send, column_recv, weight_send, weight_recv, share_send, share_recv,
    fold_send, fold_recv, line_send, line_recv, grads_send, grads_recv,
    stat_send, stat_recv, pair_send, pair_recv,
):
    group, tensor, dp = (lax.axis_index(name) for name in ("groups", "tensor", "dp"))
    bits = n_tensor.bit_length() - 1
    rows, width = first_ref.shape
    column = rows * n_tensor
    depth = w_up_ref.shape[0]
    units = w_up_ref.shape[1] // n_dp
    part = depth // n_groups
    piece = units // n_groups
    tokens = (normed_all, grad_all)
    row_sems, column_sems = (row_send, row_recv), (column_send, column_recv)
    weight_sems, share_sems = (weight_send, weight_recv), (share_send, share_recv)
    fold_sems, line_sems = (fold_send, fold_recv), (line_send, line_recv)
    grads_sems, stat_sems, pair_sems = (
        (grads_send, grads_recv), (stat_send, stat_recv), (pair_send, pair_recv),
    )

    def cut_of(z, mask):
        return span(z * n_tensor + flipped(tensor, mask, bits), rows)

    def block(a, mask, z):
        return tokens[a].at[cut_of(z, mask), :]

    def tensor_peer(bit):
        return {"tensor": flipped(tensor, 1 << bit, bits)}

    def on_line(place):
        return jnp.logical_and(place >= 0, place <= n_dp - 1)

    def peer_at(place):
        return {"dp": (place + n_dp) % n_dp}

    def row_copy(a, side, z, own):
        src = grad_ref if a == 1 and own else block(a, 0, z)
        return remote(src, block(a, 0, z), row_sems, (a, side, z), peer_at(dp + 1 - 2 * side))

    def row_side(z):
        return jnp.where(z < dp, 0, 1)

    def column_copy(a, mask, z, bit, own=False):
        src = grad_ref if a == 1 and own else block(a, mask, z)
        return remote(src, block(a, mask, z), column_sems, (a, mask | 1 << bit, z), tensor_peer(bit))

    def column_arrival(a, mask, z):
        here = block(a, mask, z)
        bit = (mask & -mask).bit_length() - 1
        return remote(here, here, column_sems, (a, mask, z), tensor_peer(bit))

    def next_bits(mask):
        top = bits if mask == 0 else (mask & -mask).bit_length() - 1
        return list(reversed(range(top)))

    through = sorted((m for m in range(1, n_tensor) if next_bits(m)), reverse=True)
    final = [m for m in range(1, n_tensor) if not next_bits(m)]

    def send_own(a):
        for side in range(2):
            pl.when(on_line(dp + 1 - 2 * side))(lambda side=side: row_copy(a, side, dp, True).start())
        for bit in next_bits(0):
            column_copy(a, 0, dp, bit, True).start()

    def row_step(z):
        side = row_side(z)
        for a in (1, 0):
            row_copy(a, side, z, False).wait_recv()
            pl.when(on_line(dp + 1 - 2 * side))(lambda a=a: row_copy(a, side, z, False).start())
            for bit in next_bits(0):
                column_copy(a, 0, z, bit).start()

    def column_step(z):
        for mask in through:
            for a in (1, 0):
                column_arrival(a, mask, z).wait_recv()
                for bit in next_bits(mask):
                    column_copy(a, mask, z, bit).start()

    def settle_step(z):
        for mask in final:
            for a in (1, 0):
                column_arrival(a, mask, z).wait_recv()

    def weight_view(kind, source, owner):
        if kind == 0:
            return up_ref.at[span(source * n_groups + owner, part), :]
        return down_ref.at[span(owner, piece), span(source, depth)]

    def weight_copy(kind, target):
        if kind == 0:
            src = w_up_ref.at[span(group, part), span(target, units)]
        else:
            src = w_down_ref.at[span(target * n_groups + group, piece), :]
        s = (target + n_dp - dp) % n_dp
        return remote(src, weight_view(kind, dp, group), weight_sems, (kind, s), {"dp": target})

    def weight_arrival(kind, source):
        here = weight_view(kind, source, group)
        s = (dp + n_dp - source) % n_dp
        return remote(here, here, weight_sems, (kind, s), {"dp": (dp + s) % n_dp})

    def share_copy(kind, source, h):
        here = weight_view(kind, source, group)
        return remote(here, here, share_sems, (kind, source, h), {"groups": (group + h) % n_groups})

    def share_arrival(kind, source, h):
        here = weight_view(kind, source, (group + n_groups - h) % n_groups)
        return remote(here, here, share_sems, (kind, source, h), {"groups": (group + h) % n_groups})

    def weight_step(kind, source):
        weight_arrival(kind, source).wait_recv()
        for h in range(1, n_groups):
            share_copy(kind, source, h).start()

    def share_step(kind):
        for k in range(1, n_dp):
            for h in range(1, n_groups):
                share_arrival(kind, near[k], h).wait_recv()

    half = column // 2

    @jax.named_scope("useup")
    def use_up(z):
        @pl.loop(0, column // half)
        def _(i):
            cut = span(z * (column // half) + i, half)
            preact = jnp.dot(normed_all[cut, :], up_ref[...], preferred_element_type=jnp.float32)
            root = (2.0 / np.pi) ** 0.5
            square = preact * preact
            bend = jnp.tanh(root * (preact + 0.044715 * (square * preact)))
            gate = 0.5 * (1.0 + bend)
            hidden_ref[cut, :] = (preact * gate).astype(hidden_ref.dtype)
            slope_ref[cut, :] = gate + (0.5 * preact) * (1.0 - bend * bend) * (
                root * (1.0 + 3.0 * 0.044715 * square)
            )

    @jax.named_scope("usedown")
    def use_down(z):
        @pl.loop(0, column // half)
        def _(i):
            cut = span(z * (column // half) + i, half)
            grad_hidden = lax.dot_general(
                grad_all[cut, :], down_ref[...], (((1,), (1,)), ((), ())),
                preferred_element_type=jnp.float32,
            )
            pre_ref[cut, :] = (grad_hidden * slope_ref[cut, :]).astype(pre_ref.dtype)

    @jax.named_scope("wblk")
    def weight_block(kind, z):
        cut = span(z, depth)
        if kind == 0:
            g_up_ref[z] = contract_tokens(normed_all[:, cut], pre_ref[...]).astype(g_up_ref.dtype)
        else:
            g_down_ref[z] = contract_tokens(hidden_ref[...], grad_all[:, cut]).astype(
                g_down_ref.dtype
            )

    def grads_view(kind, source):
        if kind == 0:
            return up_out.at[:, span(source, units)]
        return down_out.at[span(source, units), :]

    def grads_copy(kind, z):
        src = (g_up_ref, g_down_ref)[kind].at[z]
        s = (z + n_dp - dp) % n_dp
        return remote(src, grads_view(kind, dp), grads_sems, (kind, s), peer_at(z))

    def grads_arrival(kind, s):
        here = grads_view(kind, (dp + n_dp - s) % n_dp)
        return remote(here, here, grads_sems, (kind, s), {"dp": (dp + s) % n_dp})

    slots = {}
    for bit in range(bits):
        for mask in range(0, n_tensor, 2 << bit):
            slots[bit, mask] = len(slots)
    last = slots[bits - 1, 0]

    def current(a, bit, mask, z):
        if bit == 0:
            return partials.at[a, cut_of(z, mask), :]
        return fold.at[a, slots[bit - 1, mask], z]

    def fold_copy(a, bit, mask, z):
        slot = slots[bit, mask ^ 1 << bit]
        return remote(
            current(a, bit, mask, z), fold.at[a, slot, z], fold_sems, (a, slot, z), tensor_peer(bit)
        )

    def fold_arrival(a, bit, mask, z):
        slot = slots[bit, mask]
        here = fold.at[a, slot, z]
        return remote(here, here, fold_sems, (a, slot, z), tensor_peer(bit))

    def add_into(ref, other):
        @pl.loop(0, rows // 16)
        def _(i):
            cut = pl.ds(pl.multiple_of(i * 16, 16), 16)
            ref[cut, :] = (
                ref[cut, :].astype(jnp.float32) + other[cut, :].astype(jnp.float32)
            ).astype(ref.dtype)

    def sent_masks(bit):
        masks = [m for m in range(n_tensor) if m % (1 << bit) == 0 and m >> bit & 1]
        return sorted(masks, reverse=True)

    def kept_masks(bit):
        return sorted(range(0, n_tensor, 2 << bit), reverse=True)

    @jax.named_scope("mul")
    def multiply(z):
        @pl.loop(0, column // half)
        def _(i):
            cut = span(z * (column // half) + i, half)
            partials[0, cut, :] = jnp.dot(
                hidden_ref[cut, :], down_ref[...], preferred_element_type=jnp.float32
            ).astype(partials.dtype)
            partials[1, cut, :] = lax.dot_general(
                pre_ref[cut, :], up_ref[...], (((1,), (1,)), ((), ())),
                preferred_element_type=jnp.float32,
            ).astype(partials.dtype)

        for mask in sent_masks(0):
            for a in range(2):
                fold_copy(a, 0, mask, z).start()

    def folded(a, bit, mask, z):
        fold_arrival(a, bit, mask, z).wait_recv()
        add_into(fold.at[a, slots[bit, mask], z], current(a, bit, mask, z))
        if bit + 1 < bits and mask in sent_masks(bit + 1):
            fold_copy(a, bit + 1, mask, z).start()

    @jax.named_scope("inner")
    def inner_folds(z):
        for bit in range(bits - 1):
            for mask in kept_masks(bit):
                for a in range(2):
                    folded(a, bit, mask, z)

    def line_side(z):
        return jnp.where(z > dp, 0, 1)

    def line_copy(a, side, z, relayed):
        here = moving.at[side, a, z]
        src = here if relayed else fold.at[a, last, z]
        return remote(src, here, line_sems, (side, a, z), peer_at(dp + 1 - 2 * side))

    def line_arrival(a, side, z):
        here = moving.at[side, a, z]
        return remote(here, here, line_sems, (side, a, z), peer_at(dp + 1 - 2 * side))

    @jax.named_scope("fwd")
    def forward(z):
        side = line_side(z)
        behind = on_line(dp - 1 + 2 * side)
        for a in range(2):
            folded(a, bits - 1, 0, z)

            @pl.when(behind)
            def _(a=a):
                line_arrival(a, side, z).wait_recv()
                add_into(moving.at[side, a, z], fold.at[a, last, z])
                line_copy(a, side, z, True).start()

            @pl.when(jnp.logical_not(behind))
            def _(a=a):
                line_copy(a, side, z, False).start()

    near = [ranked_place(dp, n_dp, k) for k in range(n_dp)]
    far = list(reversed(near))
    early = [ranked_place(dp, n_dp, k, earliness) for k in range(n_dp)]
    inside = jnp.logical_and(on_line(dp - 1), on_line(dp + 1))

    barrier = pltpu.get_barrier_semaphore()
    peers = [{"dp": (dp + s) % n_dp} for s in range(1, n_dp)]
    peers += [tensor_peer(bit) for bit in range(bits)]
    peers += [{"groups": (group + s) % n_groups} for s in range(1, n_groups)]
    for peer in peers:
        pl.semaphore_signal(barrier, inc=1, device_id=peer, device_id_type=pl.DeviceIdType.MESH)

    local = [
        pltpu.make_async_copy(grad_ref, block(1, 0, dp), local_sem.at[1]),
        pltpu.make_async_copy(
            w_up_ref.at[:, span(dp, units)], up_ref.at[span(dp, depth), :], local_sem.at[2]
        ),
        pltpu.make_async_copy(
            w_down_ref.at[span(dp, units), :], down_ref.at[:, span(dp, depth)], local_sem.at[3]
        ),
    ]
    for copy in local:
        copy.start()

    @pl.loop(0, rows // 16)
    def _(i):
        cut = pl.ds(pl.multiple_of(i * 16, 16), 16)
        standard, _ = standardize(first_ref[cut, :])
        own_normed[cut, :] = (standard * gain_ref[...] + bias_ref[...]).astype(own_normed.dtype)

    settle = pltpu.make_async_copy(own_normed, block(0, 0, dp), local_sem.at[0])
    settle.start()
    settle.wait()
    with jax.named_scope("greet"):
        pl.semaphore_wait(barrier, len(peers))
    send_own(1)
    send_own(0)

    def weight_start(kinds, conditions):
        for kind in kinds:
            for k in range(1, n_dp):
                @pl.when(conditions(jnp.abs(near[k] - dp), inner(near[k])))
                def _(kind=kind, k=k):
                    weight_copy(kind, near[k]).start()

    def inner(z):
        return jnp.logical_and(z >= 1, z <= n_dp - 2)

    both = jnp.logical_and
    outside = jnp.logical_not(inside)
    with jax.named_scope("rows1"):
        row_step(near[1])
    weight_start((0, 1), lambda gap, to_inner: both(outside, gap == 1))
    with jax.named_scope("rows2"):
        for k in range(2, min(3, n_dp)):
            row_step(near[k])
    weight_start((0, 1), lambda gap, to_inner: both(inside, to_inner))
    weight_start((0,), lambda gap, to_inner: both(outside, gap > 1))
    with jax.named_scope("rows3"):
        for k in range(3, n_dp):
            row_step(near[k])
    weight_start((0, 1), lambda gap, to_inner: both(inside, jnp.logical_not(to_inner)))
    weight_start((1,), lambda gap, to_inner: both(outside, gap > 1))

    with jax.named_scope("cols1"):
        for k in range(n_dp - 1):
            column_step(near[k])
            if k >= 1:
                weight_step(0, early[k])
    with jax.named_scope("weights0"):
        for copy in local:
            copy.wait()
        weight_step(0, early[n_dp - 1])
        share_step(0)
    for k in range(n_dp - 1):
        with jax.named_scope("settle"):
            settle_step(near[k])
        use_up(near[k])
        if k >= 1:
            with jax.named_scope("weights1"):
                weight_step(1, early[k])
    with jax.named_scope("cols2"):
        column_step(near[n_dp - 1])
    with jax.named_scope("settle"):
        settle_step(near[n_dp - 1])
    use_up(near[n_dp - 1])

    def grads_step(kind, z):
        weight_block(kind, z)
        grads_copy(kind, z).start()

    grads_step(1, far[0])
    with jax.named_scope("weights1"):
        weight_step(1, early[n_dp - 1])
    for k in range(1, n_dp - 1):
        grads_step(1, far[k])
    with jax.named_scope("weights1"):
        share_step(1)

    for k in range(n_dp):
        use_down(far[k])
        multiply(far[k])
        if k >= 1:
            inner_folds(far[k - 1])
    inner_folds(dp)

    @pl.loop(0, n_dp)
    def _(k):
        weight_block(0, ranked_place(dp, n_dp, n_dp - 1 - k))

    def late_grads(k):
        grads_copy(0, far[k]).start()

    pl.when(inside)(lambda: late_grads(0))
    weight_block(1, dp)
    own_grads = [
        pltpu.make_async_copy(g_up_ref.at[dp], up_out.at[:, span(dp, units)], local_sem.at[0]),
        pltpu.make_async_copy(g_down_ref.at[dp], down_out.at[span(dp, units), :], local_sem.at[1]),
    ]
    for copy in own_grads:
        copy.start()
    for k in range(n_dp - 1):
        forward(far[k])
    pl.when(jnp.logical_not(inside))(lambda: late_grads(0))
    for k in range(1, n_dp - 2):
        late_grads(k)

    with jax.named_scope("last"):
        for a in range(2):
            folded(a, bits - 1, 0, dp)
            for side in range(2):
                behind = on_line(dp - 1 + 2 * side)

                @pl.when(behind)
                def _(a=a, side=side):
                    line_arrival(a, side, dp).wait_recv()

                @pl.when(jnp.logical_not(behind))
                def _(a=a, side=side):
                    moving[side, a, dp] = jnp.zeros((rows, width), moving.dtype)

    stat_line[dp] = jnp.zeros(stat_line.shape[1:], jnp.float32)

    @pl.loop(0, rows // 16)
    def _(i):
        cut = pl.ds(pl.multiple_of(i * 16, 16), 16)

        def total(a):
            return (
                fold[a, last, dp, cut, :].astype(jnp.float32)
                + moving[0, a, dp, cut, :].astype(jnp.float32)
                + moving[1, a, dp, cut, :].astype(jnp.float32)
            )

        second_in_ref[cut, :] = (second_ref[cut, :].astype(jnp.float32) - total(0)).astype(
            second_in_ref.dtype
        )
        standard, inv_std = standardize(first_ref[cut, :])
        grad_normed = total(1)
        stat_line[dp, 0:1, :] += jnp.sum(grad_normed * standard, axis=0, keepdims=True)
        stat_line[dp, 1:2, :] += jnp.sum(grad_normed, axis=0, keepdims=True)
        grad_std = grad_normed * gain_ref[...]
        grad_rows = inv_std * (
            grad_std
            - jnp.mean(grad_std, axis=-1, keepdims=True)
            - standard * jnp.mean(grad_std * standard, axis=-1, keepdims=True)
        )
        grad_first_ref[cut, :] = grad_first_in_ref[cut, :].astype(jnp.float32) + grad_rows

    def stat_copy(s):
        here = stat_line.at[dp]
        return remote(here, here, stat_sems, s, {"dp": (dp + s) % n_dp})

    def stat_arrival(s):
        here = stat_line.at[(dp + n_dp - s) % n_dp]
        return remote(here, here, stat_sems, s, {"dp": (dp + s) % n_dp})

    with jax.named_scope("stats"):
        for s in range(1, n_dp):
            stat_copy(s).start()
        for k in range(max(1, n_dp - 2), n_dp - 1):
            late_grads(k)
        for s in range(1, n_dp):
            stat_arrival(s).wait_recv()
        sums = stat_line[0]
        for source in range(1, n_dp):
            sums = sums + stat_line[source]
        for bit in range(bits):
            stat_fold[bit, 0] = sums
            copy = remote(
                stat_fold.at[bit, 0], stat_fold.at[bit, 1], pair_sems, bit, tensor_peer(bit)
            )
            copy.start()
            copy.wait()
            sums = stat_fold[bit, 0] + stat_fold[bit, 1]
        grad_norm_ref[...] = sums[0:2] * grad_scale

    with jax.named_scope("drain"):
        for s in range(1, n_dp):
            stat_copy(s).wait_send()
            for kind in range(2):
                grads_arrival(kind, s).wait_recv()
                grads_copy(kind, (dp + s) % n_dp).wait_send()
                weight_copy(kind, (dp + s) % n_dp).wait_send()
                for h in range(1, n_groups):
                    share_copy(kind, (dp + s) % n_dp, h).wait_send()
        for copy in own_grads:
            copy.wait()
        for a in range(2):
            for side in range(2):
                pl.when(on_line(dp + 1 - 2 * side))(
                    lambda a=a, side=side: row_copy(a, side, dp, True).wait_send()
                )
            for k in range(1, n_dp):
                side = row_side(near[k])
                pl.when(on_line(dp + 1 - 2 * side))(
                    lambda a=a, side=side, k=k: row_copy(a, side, near[k], False).wait_send()
                )
            for z in range(n_dp):
                for mask in [0] + through:
                    for bit in next_bits(mask):
                        column_copy(a, mask, z, bit).wait_send()
                for bit in range(bits):
                    for mask in sent_masks(bit):
                        fold_copy(a, bit, mask, z).wait_send()
            for k in range(n_dp - 1):
                line_copy(a, line_side(far[k]), far[k], True).wait_send()


ANY = pl.BlockSpec(memory_space=pl.ANY)
VMEM = pl.BlockSpec(memory_space=pltpu.VMEM)
DMA = pltpu.SemaphoreType.DMA


def spread_body(sizes, first_out, second_out, grad_first, grad_second, w_up, w_down, norm_gain, norm_bias):
    n_groups, n_tensor, n_dp = sizes
    rows, width = first_out.shape
    tokens = rows * n_tensor * n_dp
    units = w_up.shape[1] // n_dp
    bits = n_tensor.bit_length() - 1
    half = jnp.bfloat16
    grad_scale = tokens ** (-0.5)
    gain, bias = norm_gain.reshape(1, -1), norm_bias.reshape(1, -1)
    depth = w_up.shape[0]
    second_in, grad_first_in, grad_norm, up_out, down_out = pl.pallas_call(
        functools.partial(fused_kernel, n_groups, n_tensor, n_dp, grad_scale),
        out_shape=(
            jax.ShapeDtypeStruct((rows, width), half),
            jax.ShapeDtypeStruct((rows, width), jnp.float32),
            jax.ShapeDtypeStruct((2, width), jnp.float32),
            jax.ShapeDtypeStruct(w_up.shape, half),
            jax.ShapeDtypeStruct(w_down.shape, half),
        ),
        in_specs=[VMEM] * 3 + [ANY] * 3 + [VMEM] * 2,
        out_specs=(VMEM,) * 3 + (ANY,) * 2,
        scratch_shapes=[
            pltpu.VMEM((tokens, width), half),
            pltpu.VMEM((tokens, width), half),
            pltpu.VMEM((width, units), half),
            pltpu.VMEM((units, width), half),
            pltpu.VMEM((tokens, units), half),
            pltpu.VMEM((tokens, units), jnp.float32),
            pltpu.VMEM((tokens, units), half),
            pltpu.VMEM((n_dp, depth, units), half),
            pltpu.VMEM((n_dp, units, depth), half),
            pltpu.VMEM((rows, width), half),
            pltpu.VMEM((2, tokens, width), half),
            pltpu.VMEM((2, n_tensor - 1, n_dp, rows, width), half),
            pltpu.VMEM((2, 2, n_dp, rows, width), half),
            pltpu.VMEM((n_dp, 8, width), jnp.float32),
            pltpu.VMEM((bits, 2, 8, width), jnp.float32),
            DMA((4,)),
        ]
        + [DMA((2, 2, n_dp))] * 2
        + [DMA((2, n_tensor, n_dp))] * 2
        + [DMA((2, n_dp))] * 2
        + [DMA((2, n_dp, n_groups))] * 2
        + [DMA((2, n_tensor - 1, n_dp))] * 2
        + [DMA((2, 2, n_dp))] * 2
        + [DMA((2, n_dp))] * 2
        + [DMA((n_dp,))] * 2
        + [DMA((bits,))] * 2,
        compiler_params=pltpu.CompilerParams(
            collective_id=0, has_side_effects=True, vmem_limit_bytes=60 << 20
        ),
        name="spread_backward",
    )(first_out, second_out, grad_first, grad_second, w_up, w_down, gain, bias)
    grad_up = up_out.astype(jnp.float32) * grad_scale
    grad_down = down_out.astype(jnp.float32) * grad_scale
    return second_in, grad_first_in, grad_up, grad_down, grad_norm


def choose(sizes, *args):
    first_out, w_up = args[0], args[4]
    n_groups, n_tensor, n_dp = sizes
    tokens = first_out.shape[0] * n_tensor * n_dp
    fits = (
        n_tensor > 1
        and n_dp > 1
        and n_dp % 2 == 0
        and n_tensor & (n_tensor - 1) == 0
        and w_up.shape[1] % (n_dp * n_groups * 128) == 0
        and w_up.shape[0] % (n_groups * 128) == 0
    )
    if fits and tokens <= w_up.shape[1]:
        return spread_body(sizes, *args)
    return body(*args)


def solution(mesh):
    in_specs = (
        P(("groups", "tensor", "dp"), None),
        P(("groups", "tensor", "dp"), None),
        P(("groups", "tensor", "dp"), None),
        P(("groups", "tensor", "dp"), None),
        P("dp", "tensor"),
        P("tensor", "dp"),
        P(),
        P(),
    )
    out_specs = (
        P(("groups", "tensor", "dp"), None),
        P(("groups", "tensor", "dp"), None),
        P(("groups", "dp"), "tensor"),
        P(("groups", "tensor"), "dp"),
        P("groups", None),
    )
    sizes = tuple(mesh.shape[name] for name in ("groups", "tensor", "dp"))
    return jax.shard_map(functools.partial(choose, sizes), mesh=mesh, in_specs=in_specs, out_specs=out_specs, check_vma=False)
```

```python
import functools

import jax
import jax.numpy as jnp
import numpy as np
from jax import lax
from jax.experimental import pallas as pl
from jax.experimental.pallas import tpu as pltpu
from jax.sharding import PartitionSpec as P

epsilon = 1e-06


def normalize(row_data, norm_gain, norm_bias):
    values = row_data.astype(jnp.float32)
    row_mean = jnp.mean(values, axis=-1, keepdims=True)
    centred = values - row_mean
    inv_std = lax.rsqrt(jnp.mean(centred * centred, axis=-1, keepdims=True) + epsilon)
    standard = centred * inv_std
    normed = (standard * norm_gain + norm_bias).astype(jnp.bfloat16)
    return (standard, inv_std, normed)


def contract_tokens(left_rows, right_rows):
    return lax.dot_general(
        left_rows, right_rows, (((0,), (0,)), ((), ())), preferred_element_type=jnp.float32
    )


def body(first_out, second_out, grad_first, grad_second, w_up, w_down, norm_gain, norm_bias):
    own_rows = first_out.shape[0]
    up_full, down_full = (
        lax.all_gather(w_up, "dp", axis=0, tiled=True),
        lax.all_gather(w_down, "dp", axis=1, tiled=True),
    )
    first_all, grad_all = (
        lax.all_gather(first_out, "tensor", axis=0, tiled=True),
        lax.all_gather(grad_second, "tensor", axis=0, tiled=True),
    )
    standard_all, inv_std_all, normed = normalize(first_all, norm_gain, norm_bias)
    offset = lax.axis_index("tensor") * own_rows
    standard = lax.dynamic_slice_in_dim(standard_all, offset, own_rows, 0)
    inv_std = lax.dynamic_slice_in_dim(inv_std_all, offset, own_rows, 0)
    preact = jnp.dot(normed, up_full, preferred_element_type=jnp.float32)
    hidden = jax.nn.gelu(preact).astype(jnp.bfloat16)
    branch = lax.psum_scatter(
        jnp.dot(hidden, down_full, preferred_element_type=jnp.float32).astype(jnp.bfloat16),
        "tensor",
        scatter_dimension=0,
        tiled=True,
    ).astype(jnp.float32)
    second_in = (second_out.astype(jnp.float32) - branch).astype(jnp.bfloat16)
    tokens = own_rows * lax.axis_size("tensor") * lax.axis_size("dp")
    grad_scale = tokens ** (-0.5)
    grad_down_part = contract_tokens(hidden, grad_all)
    grad_down = (
        lax.psum_scatter(
            grad_down_part.astype(jnp.bfloat16), "dp", scatter_dimension=1, tiled=True
        ).astype(jnp.float32)
        * grad_scale
    )
    grad_hidden = lax.dot_general(
        grad_all, down_full, (((1,), (1,)), ((), ())), preferred_element_type=jnp.float32
    )
    grad_pre = jax.vjp(jax.nn.gelu, preact)[1](grad_hidden)[0].astype(jnp.bfloat16)
    grad_up_part = contract_tokens(normed, grad_pre)
    grad_up = (
        lax.psum_scatter(
            grad_up_part.astype(jnp.bfloat16), "dp", scatter_dimension=0, tiled=True
        ).astype(jnp.float32)
        * grad_scale
    )
    grad_normed = lax.psum_scatter(
        lax.dot_general(
            grad_pre, up_full, (((1,), (1,)), ((), ())), preferred_element_type=jnp.float32
        ).astype(jnp.bfloat16),
        "tensor",
        scatter_dimension=0,
        tiled=True,
    ).astype(jnp.float32)
    grad_std = grad_normed * norm_gain
    grad_rows = inv_std * (
        grad_std
        - jnp.mean(grad_std, axis=-1, keepdims=True)
        - standard * jnp.mean(grad_std * standard, axis=-1, keepdims=True)
    )
    grad_first_in = grad_first.astype(jnp.float32) + grad_rows
    local_stats = jnp.stack([jnp.sum(grad_normed * standard, axis=0), jnp.sum(grad_normed, axis=0)])
    grad_norm = lax.psum(local_stats, ("tensor", "dp")) * grad_scale
    return (second_in, grad_first_in, grad_up, grad_down, grad_norm)


def span(index, size):
    return pl.ds(pl.multiple_of(index * size, size), size)


def flipped(index, mask, bits):
    for bit in range(bits):
        if mask >> bit & 1:
            step = 1 << bit
            index = index + (1 - 2 * ((index // step) % 2)) * step
    return index


def nearness(own, n_dp):
    return lambda z: (abs(z - own), z)


def earliness(own, n_dp):
    def key(z):
        edge = min(z, n_dp - 1 - z)
        return (z != own, edge, abs(z - own) if edge == 0 else -abs(z - own))

    return key


def ranked_place(dp, n_dp, rank, ranking=nearness):
    place = 0
    for own in range(n_dp):
        ranked = sorted(range(n_dp), key=ranking(own, n_dp))
        for k in range(n_dp):
            here = jnp.logical_and(dp == own, jnp.equal(rank, k))
            place = place + jnp.where(here, ranked[k], 0)
    return place


def remote(src, dst, sems, index, peer):
    return pltpu.make_async_remote_copy(
        src_ref=src,
        dst_ref=dst,
        send_sem=sems[0].at[index],
        recv_sem=sems[1].at[index],
        device_id=peer,
        device_id_type=pl.DeviceIdType.MESH,
    )


def standardize(row_data):
    values = row_data.astype(jnp.float32)
    centred = values - jnp.mean(values, axis=-1, keepdims=True)
    inv_std = lax.rsqrt(jnp.mean(centred * centred, axis=-1, keepdims=True) + epsilon)
    return centred * inv_std, inv_std


def fused_kernel(
    n_groups, n_tensor, n_dp, grad_scale,
    first_ref, second_ref, grad_first_in_ref, grad_ref, w_up_ref, w_down_ref, gain_ref, bias_ref,
    second_in_ref, grad_first_ref, grad_norm_ref, up_out, down_out,
    normed_all, grad_all, up_ref, down_ref, hidden_ref, slope_ref, pre_ref, g_up_ref, g_down_ref, own_normed,
    partials, fold, moving, stat_line, stat_fold, local_sem,
    row_send, row_recv, column_send, column_recv, weight_send, weight_recv, share_send, share_recv,
    fold_send, fold_recv, line_send, line_recv, grads_send, grads_recv,
    stat_send, stat_recv, pair_send, pair_recv,
):
    group, tensor, dp = (lax.axis_index(name) for name in ("groups", "tensor", "dp"))
    bits = n_tensor.bit_length() - 1
    rows, width = first_ref.shape
    column = rows * n_tensor
    depth = w_up_ref.shape[0]
    units = w_up_ref.shape[1] // n_dp
    part = depth // n_groups
    piece = units // n_groups
    tokens = (normed_all, grad_all)
    row_sems, column_sems = (row_send, row_recv), (column_send, column_recv)
    weight_sems, share_sems = (weight_send, weight_recv), (share_send, share_recv)
    fold_sems, line_sems = (fold_send, fold_recv), (line_send, line_recv)
    grads_sems, stat_sems, pair_sems = (
        (grads_send, grads_recv), (stat_send, stat_recv), (pair_send, pair_recv),
    )

    def cut_of(z, mask):
        return span(z * n_tensor + flipped(tensor, mask, bits), rows)

    def block(a, mask, z):
        return tokens[a].at[cut_of(z, mask), :]

    def tensor_peer(bit):
        return {"tensor": flipped(tensor, 1 << bit, bits)}

    def on_line(place):
        return jnp.logical_and(place >= 0, place <= n_dp - 1)

    def peer_at(place):
        return {"dp": (place + n_dp) % n_dp}

    def row_copy(a, side, z, own):
        src = grad_ref if a == 1 and own else block(a, 0, z)
        return remote(src, block(a, 0, z), row_sems, (a, side, z), peer_at(dp + 1 - 2 * side))

    def row_side(z):
        return jnp.where(z < dp, 0, 1)

    def column_copy(a, mask, z, bit, own=False):
        src = grad_ref if a == 1 and own else block(a, mask, z)
        return remote(src, block(a, mask, z), column_sems, (a, mask | 1 << bit, z), tensor_peer(bit))

    def column_arrival(a, mask, z):
        here = block(a, mask, z)
        bit = (mask & -mask).bit_length() - 1
        return remote(here, here, column_sems, (a, mask, z), tensor_peer(bit))

    def next_bits(mask):
        top = bits if mask == 0 else (mask & -mask).bit_length() - 1
        return list(reversed(range(top)))

    through = sorted((m for m in range(1, n_tensor) if next_bits(m)), reverse=True)
    final = [m for m in range(1, n_tensor) if not next_bits(m)]

    def send_own(a):
        for side in range(2):
            pl.when(on_line(dp + 1 - 2 * side))(lambda side=side: row_copy(a, side, dp, True).start())
        for bit in next_bits(0):
            column_copy(a, 0, dp, bit, True).start()

    def row_step(z):
        side = row_side(z)
        for a in (1, 0):
            row_copy(a, side, z, False).wait_recv()
            pl.when(on_line(dp + 1 - 2 * side))(lambda a=a: row_copy(a, side, z, False).start())
            for bit in next_bits(0):
                column_copy(a, 0, z, bit).start()

    def column_step(z):
        for mask in through:
            for a in (1, 0):
                column_arrival(a, mask, z).wait_recv()
                for bit in next_bits(mask):
                    column_copy(a, mask, z, bit).start()

    def settle_step(z):
        for mask in final:
            for a in (1, 0):
                column_arrival(a, mask, z).wait_recv()

    def weight_view(kind, source, owner):
        if kind == 0:
            return up_ref.at[span(source * n_groups + owner, part), :]
        return down_ref.at[span(owner, piece), span(source, depth)]

    def weight_copy(kind, target):
        if kind == 0:
            src = w_up_ref.at[span(group, part), span(target, units)]
        else:
            src = w_down_ref.at[span(target * n_groups + group, piece), :]
        s = (target + n_dp - dp) % n_dp
        return remote(src, weight_view(kind, dp, group), weight_sems, (kind, s), {"dp": target})

    def weight_arrival(kind, source):
        here = weight_view(kind, source, group)
        s = (dp + n_dp - source) % n_dp
        return remote(here, here, weight_sems, (kind, s), {"dp": (dp + s) % n_dp})

    def share_copy(kind, source, h):
        here = weight_view(kind, source, group)
        return remote(here, here, share_sems, (kind, source, h), {"groups": (group + h) % n_groups})

    def share_arrival(kind, source, h):
        here = weight_view(kind, source, (group + n_groups - h) % n_groups)
        return remote(here, here, share_sems, (kind, source, h), {"groups": (group + h) % n_groups})

    def weight_step(kind, source):
        weight_arrival(kind, source).wait_recv()
        for h in range(1, n_groups):
            share_copy(kind, source, h).start()

    def share_step(kind):
        for k in range(1, n_dp):
            for h in range(1, n_groups):
                share_arrival(kind, near[k], h).wait_recv()

    half = column // 2

    @jax.named_scope("useup")
    def use_up(z):
        @pl.loop(0, column // half)
        def _(i):
            cut = span(z * (column // half) + i, half)
            preact = jnp.dot(normed_all[cut, :], up_ref[...], preferred_element_type=jnp.float32)
            root = (2.0 / np.pi) ** 0.5
            square = preact * preact
            bend = jnp.tanh(root * (preact + 0.044715 * (square * preact)))
            gate = 0.5 * (1.0 + bend)
            hidden_ref[cut, :] = (preact * gate).astype(hidden_ref.dtype)
            slope_ref[cut, :] = gate + (0.5 * preact) * (1.0 - bend * bend) * (
                root * (1.0 + 3.0 * 0.044715 * square)
            )

    @jax.named_scope("usedown")
    def use_down(z):
        @pl.loop(0, column // half)
        def _(i):
            cut = span(z * (column // half) + i, half)
            grad_hidden = lax.dot_general(
                grad_all[cut, :], down_ref[...], (((1,), (1,)), ((), ())),
                preferred_element_type=jnp.float32,
            )
            pre_ref[cut, :] = (grad_hidden * slope_ref[cut, :]).astype(pre_ref.dtype)

    @jax.named_scope("wblk")
    def weight_block(kind, z):
        cut = span(z, depth)
        if kind == 0:
            g_up_ref[z] = contract_tokens(normed_all[:, cut], pre_ref[...]).astype(g_up_ref.dtype)
        else:
            g_down_ref[z] = contract_tokens(hidden_ref[...], grad_all[:, cut]).astype(
                g_down_ref.dtype
            )

    def grads_view(kind, source):
        if kind == 0:
            return up_out.at[:, span(source, units)]
        return down_out.at[span(source, units), :]

    def grads_copy(kind, z):
        src = (g_up_ref, g_down_ref)[kind].at[z]
        s = (z + n_dp - dp) % n_dp
        return remote(src, grads_view(kind, dp), grads_sems, (kind, s), peer_at(z))

    def grads_arrival(kind, s):
        here = grads_view(kind, (dp + n_dp - s) % n_dp)
        return remote(here, here, grads_sems, (kind, s), {"dp": (dp + s) % n_dp})

    slots = {}
    for bit in range(bits):
        for mask in range(0, n_tensor, 2 << bit):
            slots[bit, mask] = len(slots)
    last = slots[bits - 1, 0]

    def current(a, bit, mask, z):
        if bit == 0:
            return partials.at[a, cut_of(z, mask), :]
        return fold.at[a, slots[bit - 1, mask], z]

    def fold_copy(a, bit, mask, z):
        slot = slots[bit, mask ^ 1 << bit]
        return remote(
            current(a, bit, mask, z), fold.at[a, slot, z], fold_sems, (a, slot, z), tensor_peer(bit)
        )

    def fold_arrival(a, bit, mask, z):
        slot = slots[bit, mask]
        here = fold.at[a, slot, z]
        return remote(here, here, fold_sems, (a, slot, z), tensor_peer(bit))

    def add_into(ref, other):
        @pl.loop(0, rows // 16)
        def _(i):
            cut = pl.ds(pl.multiple_of(i * 16, 16), 16)
            ref[cut, :] = (
                ref[cut, :].astype(jnp.float32) + other[cut, :].astype(jnp.float32)
            ).astype(ref.dtype)

    def sent_masks(bit):
        masks = [m for m in range(n_tensor) if m % (1 << bit) == 0 and m >> bit & 1]
        return sorted(masks, reverse=True)

    def kept_masks(bit):
        return sorted(range(0, n_tensor, 2 << bit), reverse=True)

    @jax.named_scope("mul")
    def multiply(z):
        @pl.loop(0, column // half)
        def _(i):
            cut = span(z * (column // half) + i, half)
            partials[0, cut, :] = jnp.dot(
                hidden_ref[cut, :], down_ref[...], preferred_element_type=jnp.float32
            ).astype(partials.dtype)
            partials[1, cut, :] = lax.dot_general(
                pre_ref[cut, :], up_ref[...], (((1,), (1,)), ((), ())),
                preferred_element_type=jnp.float32,
            ).astype(partials.dtype)

        for mask in sent_masks(0):
            for a in range(2):
                fold_copy(a, 0, mask, z).start()

    def folded(a, bit, mask, z):
        fold_arrival(a, bit, mask, z).wait_recv()
        add_into(fold.at[a, slots[bit, mask], z], current(a, bit, mask, z))
        if bit + 1 < bits and mask in sent_masks(bit + 1):
            fold_copy(a, bit + 1, mask, z).start()

    @jax.named_scope("inner")
    def inner_folds(z):
        for bit in range(bits - 1):
            for mask in kept_masks(bit):
                for a in range(2):
                    folded(a, bit, mask, z)

    def line_side(z):
        return jnp.where(z > dp, 0, 1)

    def line_copy(a, side, z, relayed):
        here = moving.at[side, a, z]
        src = here if relayed else fold.at[a, last, z]
        return remote(src, here, line_sems, (side, a, z), peer_at(dp + 1 - 2 * side))

    def line_arrival(a, side, z):
        here = moving.at[side, a, z]
        return remote(here, here, line_sems, (side, a, z), peer_at(dp + 1 - 2 * side))

    @jax.named_scope("fwd")
    def forward(z):
        side = line_side(z)
        behind = on_line(dp - 1 + 2 * side)
        for a in range(2):
            folded(a, bits - 1, 0, z)

            @pl.when(behind)
            def _(a=a):
                line_arrival(a, side, z).wait_recv()
                add_into(moving.at[side, a, z], fold.at[a, last, z])
                line_copy(a, side, z, True).start()

            @pl.when(jnp.logical_not(behind))
            def _(a=a):
                line_copy(a, side, z, False).start()

    near = [ranked_place(dp, n_dp, k) for k in range(n_dp)]
    far = list(reversed(near))
    early = [ranked_place(dp, n_dp, k, earliness) for k in range(n_dp)]
    inside = jnp.logical_and(on_line(dp - 1), on_line(dp + 1))

    barrier = pltpu.get_barrier_semaphore()
    peers = [{"dp": (dp + s) % n_dp} for s in range(1, n_dp)]
    peers += [tensor_peer(bit) for bit in range(bits)]
    peers += [{"groups": (group + s) % n_groups} for s in range(1, n_groups)]
    for peer in peers:
        pl.semaphore_signal(barrier, inc=1, device_id=peer, device_id_type=pl.DeviceIdType.MESH)

    local = [
        pltpu.make_async_copy(grad_ref, block(1, 0, dp), local_sem.at[1]),
        pltpu.make_async_copy(
            w_up_ref.at[:, span(dp, units)], up_ref.at[span(dp, depth), :], local_sem.at[2]
        ),
        pltpu.make_async_copy(
            w_down_ref.at[span(dp, units), :], down_ref.at[:, span(dp, depth)], local_sem.at[3]
        ),
    ]
    for copy in local:
        copy.start()

    @pl.loop(0, rows // 16)
    def _(i):
        cut = pl.ds(pl.multiple_of(i * 16, 16), 16)
        standard, _ = standardize(first_ref[cut, :])
        own_normed[cut, :] = (standard * gain_ref[...] + bias_ref[...]).astype(own_normed.dtype)

    settle = pltpu.make_async_copy(own_normed, block(0, 0, dp), local_sem.at[0])
    settle.start()
    settle.wait()
    with jax.named_scope("greet"):
        pl.semaphore_wait(barrier, len(peers))
    send_own(1)
    send_own(0)

    def weight_start(kinds, conditions):
        for kind in kinds:
            for k in range(1, n_dp):
                @pl.when(conditions(jnp.abs(near[k] - dp), inner(near[k])))
                def _(kind=kind, k=k):
                    weight_copy(kind, near[k]).start()

    def inner(z):
        return jnp.logical_and(z >= 1, z <= n_dp - 2)

    both = jnp.logical_and
    outside = jnp.logical_not(inside)
    with jax.named_scope("rows1"):
        row_step(near[1])
    weight_start((0, 1), lambda gap, to_inner: both(outside, gap == 1))
    with jax.named_scope("rows2"):
        for k in range(2, min(3, n_dp)):
            row_step(near[k])
    weight_start((0, 1), lambda gap, to_inner: both(inside, to_inner))
    weight_start((0, 1), lambda gap, to_inner: both(inside, both(gap == 1, jnp.logical_not(to_inner))))
    weight_start((0,), lambda gap, to_inner: both(outside, gap > 1))

    def far_rows():
        with jax.named_scope("rows3"):
            for k in range(3, n_dp):
                row_step(near[k])

    pl.when(inside)(far_rows)
    weight_start((), lambda gap, to_inner: both(inside, both(gap == 1, jnp.logical_not(to_inner))))
    weight_start((0, 1), lambda gap, to_inner: both(inside, both(gap > 1, jnp.logical_not(to_inner))))
    with jax.named_scope("cols1"):
        column_step(near[0])
        weight_step(0, early[1])
        for k in range(1, n_dp - 1):
            column_step(near[k])
        for k in range(2, n_dp):
            weight_step(0, early[k])
    weight_start((1,), lambda gap, to_inner: both(outside, gap > 1))
    last_one = jnp.where(inside, early[n_dp - 2], early[1])
    with jax.named_scope("weights0"):
        for copy in local:
            copy.wait()
        for k in range(1, n_dp):
            pl.when(early[k] != last_one)(lambda k=k: weight_step(1, early[k]))
        share_step(0)
    for k in range(n_dp - 1):
        with jax.named_scope("settle"):
            settle_step(near[k])
        use_up(near[k])
    def own_partial():
        with jax.named_scope("weights1"):
            share_step(1)
        use_down(dp)
        multiply(dp)
        inner_folds(dp)

    @pl.when(outside)
    def _():
        weight_step(1, last_one)
        far_rows()
        own_partial()

    with jax.named_scope("cols2"):
        column_step(near[n_dp - 1])
    pl.when(inside)(lambda: weight_step(1, last_one))
    with jax.named_scope("settle"):
        settle_step(near[n_dp - 1])
    use_up(near[n_dp - 1])

    def grads_step(kind, z):
        weight_block(kind, z)
        grads_copy(kind, z).start()

    for k in range(n_dp - 1):
        grads_step(1, far[k])
    pl.when(inside)(own_partial)
    for k in range(n_dp - 1):
        use_down(far[k])
        multiply(far[k])
        if k >= 1:
            inner_folds(far[k - 1])
    inner_folds(far[n_dp - 2])

    @pl.loop(0, n_dp)
    def _(k):
        weight_block(0, ranked_place(dp, n_dp, n_dp - 1 - k))

    def late_grads(k):
        grads_copy(0, far[k]).start()

    pl.when(inside)(lambda: late_grads(0))
    weight_block(1, dp)
    own_grads = [
        pltpu.make_async_copy(g_up_ref.at[dp], up_out.at[:, span(dp, units)], local_sem.at[0]),
        pltpu.make_async_copy(g_down_ref.at[dp], down_out.at[span(dp, units), :], local_sem.at[1]),
    ]
    for copy in own_grads:
        copy.start()
    for k in range(n_dp - 1):
        forward(far[k])
    pl.when(jnp.logical_not(inside))(lambda: late_grads(0))
    for k in range(1, n_dp - 2):
        late_grads(k)

    with jax.named_scope("last"):
        for a in range(2):
            folded(a, bits - 1, 0, dp)
            for side in range(2):
                behind = on_line(dp - 1 + 2 * side)

                @pl.when(behind)
                def _(a=a, side=side):
                    line_arrival(a, side, dp).wait_recv()

                @pl.when(jnp.logical_not(behind))
                def _(a=a, side=side):
                    moving[side, a, dp] = jnp.zeros((rows, width), moving.dtype)

    stat_line[dp] = jnp.zeros(stat_line.shape[1:], jnp.float32)

    @pl.loop(0, rows // 16)
    def _(i):
        cut = pl.ds(pl.multiple_of(i * 16, 16), 16)

        def total(a):
            return (
                fold[a, last, dp, cut, :].astype(jnp.float32)
                + moving[0, a, dp, cut, :].astype(jnp.float32)
                + moving[1, a, dp, cut, :].astype(jnp.float32)
            )

        second_in_ref[cut, :] = (second_ref[cut, :].astype(jnp.float32) - total(0)).astype(
            second_in_ref.dtype
        )
        standard, inv_std = standardize(first_ref[cut, :])
        grad_normed = total(1)
        stat_line[dp, 0:1, :] += jnp.sum(grad_normed * standard, axis=0, keepdims=True)
        stat_line[dp, 1:2, :] += jnp.sum(grad_normed, axis=0, keepdims=True)
        grad_std = grad_normed * gain_ref[...]
        grad_rows = inv_std * (
            grad_std
            - jnp.mean(grad_std, axis=-1, keepdims=True)
            - standard * jnp.mean(grad_std * standard, axis=-1, keepdims=True)
        )
        grad_first_ref[cut, :] = grad_first_in_ref[cut, :].astype(jnp.float32) + grad_rows

    def stat_copy(s):
        here = stat_line.at[dp]
        return remote(here, here, stat_sems, s, {"dp": (dp + s) % n_dp})

    def stat_arrival(s):
        here = stat_line.at[(dp + n_dp - s) % n_dp]
        return remote(here, here, stat_sems, s, {"dp": (dp + s) % n_dp})

    with jax.named_scope("stats"):
        for s in range(1, n_dp):
            stat_copy(s).start()
        for k in range(max(1, n_dp - 2), n_dp - 1):
            late_grads(k)
        for s in range(1, n_dp):
            stat_arrival(s).wait_recv()
        sums = stat_line[0]
        for source in range(1, n_dp):
            sums = sums + stat_line[source]
        for bit in range(bits):
            stat_fold[bit, 0] = sums
            copy = remote(
                stat_fold.at[bit, 0], stat_fold.at[bit, 1], pair_sems, bit, tensor_peer(bit)
            )
            copy.start()
            copy.wait()
            sums = stat_fold[bit, 0] + stat_fold[bit, 1]
        grad_norm_ref[...] = sums[0:2] * grad_scale

    with jax.named_scope("drain"):
        for s in range(1, n_dp):
            stat_copy(s).wait_send()
            for kind in range(2):
                grads_arrival(kind, s).wait_recv()
                grads_copy(kind, (dp + s) % n_dp).wait_send()
                weight_copy(kind, (dp + s) % n_dp).wait_send()
                for h in range(1, n_groups):
                    share_copy(kind, (dp + s) % n_dp, h).wait_send()
        for copy in own_grads:
            copy.wait()
        for a in range(2):
            for side in range(2):
                pl.when(on_line(dp + 1 - 2 * side))(
                    lambda a=a, side=side: row_copy(a, side, dp, True).wait_send()
                )
            for k in range(1, n_dp):
                side = row_side(near[k])
                pl.when(on_line(dp + 1 - 2 * side))(
                    lambda a=a, side=side, k=k: row_copy(a, side, near[k], False).wait_send()
                )
            for z in range(n_dp):
                for mask in [0] + through:
                    for bit in next_bits(mask):
                        column_copy(a, mask, z, bit).wait_send()
                for bit in range(bits):
                    for mask in sent_masks(bit):
                        fold_copy(a, bit, mask, z).wait_send()
            for k in range(n_dp - 1):
                line_copy(a, line_side(far[k]), far[k], True).wait_send()


ANY = pl.BlockSpec(memory_space=pl.ANY)
VMEM = pl.BlockSpec(memory_space=pltpu.VMEM)
DMA = pltpu.SemaphoreType.DMA


def spread_body(sizes, first_out, second_out, grad_first, grad_second, w_up, w_down, norm_gain, norm_bias):
    n_groups, n_tensor, n_dp = sizes
    rows, width = first_out.shape
    tokens = rows * n_tensor * n_dp
    units = w_up.shape[1] // n_dp
    bits = n_tensor.bit_length() - 1
    half = jnp.bfloat16
    grad_scale = tokens ** (-0.5)
    gain, bias = norm_gain.reshape(1, -1), norm_bias.reshape(1, -1)
    depth = w_up.shape[0]
    second_in, grad_first_in, grad_norm, up_out, down_out = pl.pallas_call(
        functools.partial(fused_kernel, n_groups, n_tensor, n_dp, grad_scale),
        out_shape=(
            jax.ShapeDtypeStruct((rows, width), half),
            jax.ShapeDtypeStruct((rows, width), jnp.float32),
            jax.ShapeDtypeStruct((2, width), jnp.float32),
            jax.ShapeDtypeStruct(w_up.shape, half),
            jax.ShapeDtypeStruct(w_down.shape, half),
        ),
        in_specs=[VMEM] * 3 + [ANY] * 3 + [VMEM] * 2,
        out_specs=(VMEM,) * 3 + (ANY,) * 2,
        scratch_shapes=[
            pltpu.VMEM((tokens, width), half),
            pltpu.VMEM((tokens, width), half),
            pltpu.VMEM((width, units), half),
            pltpu.VMEM((units, width), half),
            pltpu.VMEM((tokens, units), half),
            pltpu.VMEM((tokens, units), jnp.float32),
            pltpu.VMEM((tokens, units), half),
            pltpu.VMEM((n_dp, depth, units), half),
            pltpu.VMEM((n_dp, units, depth), half),
            pltpu.VMEM((rows, width), half),
            pltpu.VMEM((2, tokens, width), half),
            pltpu.VMEM((2, n_tensor - 1, n_dp, rows, width), half),
            pltpu.VMEM((2, 2, n_dp, rows, width), half),
            pltpu.VMEM((n_dp, 8, width), jnp.float32),
            pltpu.VMEM((bits, 2, 8, width), jnp.float32),
            DMA((4,)),
        ]
        + [DMA((2, 2, n_dp))] * 2
        + [DMA((2, n_tensor, n_dp))] * 2
        + [DMA((2, n_dp))] * 2
        + [DMA((2, n_dp, n_groups))] * 2
        + [DMA((2, n_tensor - 1, n_dp))] * 2
        + [DMA((2, 2, n_dp))] * 2
        + [DMA((2, n_dp))] * 2
        + [DMA((n_dp,))] * 2
        + [DMA((bits,))] * 2,
        compiler_params=pltpu.CompilerParams(
            collective_id=0, has_side_effects=True, vmem_limit_bytes=60 << 20
        ),
        name="spread_backward",
    )(first_out, second_out, grad_first, grad_second, w_up, w_down, gain, bias)
    grad_up = up_out.astype(jnp.float32) * grad_scale
    grad_down = down_out.astype(jnp.float32) * grad_scale
    return second_in, grad_first_in, grad_up, grad_down, grad_norm


def choose(sizes, *args):
    first_out, w_up = args[0], args[4]
    n_groups, n_tensor, n_dp = sizes
    tokens = first_out.shape[0] * n_tensor * n_dp
    fits = (
        n_tensor > 1
        and n_dp > 1
        and n_dp % 2 == 0
        and n_tensor & (n_tensor - 1) == 0
        and w_up.shape[1] % (n_dp * n_groups * 128) == 0
        and w_up.shape[0] % (n_groups * 128) == 0
    )
    if fits and tokens <= w_up.shape[1]:
        return spread_body(sizes, *args)
    return body(*args)


def solution(mesh):
    in_specs = (
        P(("groups", "tensor", "dp"), None),
        P(("groups", "tensor", "dp"), None),
        P(("groups", "tensor", "dp"), None),
        P(("groups", "tensor", "dp"), None),
        P("dp", "tensor"),
        P("tensor", "dp"),
        P(),
        P(),
    )
    out_specs = (
        P(("groups", "tensor", "dp"), None),
        P(("groups", "tensor", "dp"), None),
        P(("groups", "dp"), "tensor"),
        P(("groups", "tensor"), "dp"),
        P("groups", None),
    )
    sizes = tuple(mesh.shape[name] for name in ("groups", "tensor", "dp"))
    return jax.shard_map(functools.partial(choose, sizes), mesh=mesh, in_specs=in_specs, out_specs=out_specs, check_vma=False)
```
